128 devices in a mesh: loop: 4 (over z_hi, core), blk: 32 (over z_lo, y, x).
Axes of the slice: x: 4, y: 4, z: 4 (z_hi: 2, z_lo: 2; z = z_hi * 2 + z_lo), core: 2. Of those that a mesh axis runs over, the one named last changes fastest.
Arguments:
- user_factors: float32 [4, 32, 1024, 512], P('loop', 'blk'), may hold values from -0.4 to 0.4
- blocks: float32 [4, 32, 2, 512, 512], P('loop', 'blk'), may hold values from -0.4 to 0.4
- user_tile: int32 [4, 32, 4, 12], P('loop', 'blk'), may hold values from 0 to 7
- item_tile: int32 [4, 32, 4, 12], P('loop', 'blk'), may hold values from 0 to 7
- ratings: bfloat16 [4, 32, 4, 12, 128, 128], P('loop', 'blk'), may hold values from -6 to 6
- dest_loop: int32 [4, 32, 2], P(None, 'blk'), may hold values from 0 to 3, as said below
Outputs:
- user_result: float32 [4, 32, 1024, 512], P('loop', 'blk')
- block_result: float32 [4, 32, 2, 512, 512], P('loop', 'blk')
The draws below stay inside these ranges and needn't reach their ends.
Inputs may be any that keep to these rules, and one draw needn't show every extreme that they name: `dest_loop`: for each shard index c: every loop receives exactly 2 blocks of index c; two loops send both their blocks to one loop each, and the other two loops each send one block to each of the two remaining loops.
All inputs are finite; a program needn't handle non-finite values.
Results may differ from the reference program's by a relative error of at most 0.0003.
Values sent between devices are 32-bit elements; how exact they have to be, the bound alone decides.
No kernel may reach another device: no remote copies, remote signals or barrier semaphores. Data moves between devices by JAX's collectives and lax.ppermute only.
A program may use at most 128 MiB of HBM per device.

```python
import jax
import jax.numpy as jnp
from jax import lax

RANK = 512
TILE = 128
UD = 1024
IB = 512
S = 2
VISITS = 4
SLOTS = 12
LOOPS = 4
COLS = 32
UT = 8
IT = 8


def factor_draw(base_key, array_shape):
    key_main = jax.random.fold_in(base_key, 0)
    samples = jax.random.truncated_normal(key_main, -4.0, 4.0, array_shape, jnp.float32)
    return (0.1 * samples).astype(jnp.float32)


def draw_user_factors(key, part):
    return factor_draw(jax.random.fold_in(key, 11), (LOOPS, COLS, UD, RANK))


def draw_blocks(key, part):
    return factor_draw(jax.random.fold_in(key, 13), (LOOPS, COLS, S, IB, RANK))


def column_routes(column_key):
    key_order, key_target, key_flip = jax.random.split(column_key, 3)
    senders = jax.random.permutation(key_order, LOOPS).astype(jnp.int32)
    targets = jax.random.permutation(key_target, LOOPS).astype(jnp.int32)
    flip_slots = jax.random.randint(key_flip, (LOOPS,), 0, S).astype(jnp.int32)
    loop_iota = jnp.arange(LOOPS, dtype=jnp.int32)
    sender_place = jnp.sum(jnp.where(senders[None, :] == loop_iota[:, None], loop_iota[None, :], 0), axis=1).astype(jnp.int32)
    slot_iota = jnp.arange(S, dtype=jnp.int32)
    whole_target = jnp.take(targets, jnp.minimum(sender_place, 1))
    split_target = jnp.where(slot_iota[None, :] == flip_slots[:, None], targets[2], targets[3])
    return jnp.where(sender_place[:, None] < 2, whole_target[:, None], split_target).astype(jnp.int32)


def draw_dest_loop(key, part):
    column_keys = jax.random.split(jax.random.fold_in(key, 7), COLS)
    return jnp.transpose(jax.vmap(column_routes)(column_keys), (1, 0, 2)).astype(jnp.int32)


def with_ends(drawn, rng, smallest, largest):
    place = [jax.random.randint(jax.random.fold_in(rng, axis), (), 0, length) for axis, length in enumerate(drawn.shape)]
    longest = drawn.shape.index(max(drawn.shape))
    beside = place[:longest] + [(place[longest] + 1) % drawn.shape[longest]] + place[longest + 1:]
    return drawn.at[tuple(place)].set(smallest).at[tuple(beside)].set(largest)


def shard_levels(key, shape, shards, least, top_value):
    def one(axis_at, blocks):
        steps = jax.random.uniform(jax.random.fold_in(jax.random.fold_in(key, 6), axis_at), (blocks,), jnp.float32, least / len(shards), top_value / len(shards))
        return jnp.repeat(jnp.exp(steps), shape[axis_at] // blocks).reshape((-1,) + (1,) * (len(shape) - axis_at - 1))

    loudness = one(*shards[0])
    for cut in shards[1:]:
        loudness = loudness * one(*cut)
    return loudness


def bell_draw(own_key, extent, deviation, most, cuts=(), held_as=jnp.bfloat16):
    drawn = jax.random.normal(own_key, extent, jnp.float32) * deviation
    if len(cuts) > 0:
        drawn = shard_levels(own_key, extent, cuts, -0.22, 0.18) * drawn
    return jnp.clip(drawn, min=-most, max=most).astype(held_as)


def setup_inputs(seed: int = 0) -> dict:
    splits = jax.random.split(jax.random.key(seed), 7)
    user_factors = draw_user_factors(jax.random.fold_in(splits[6], 71), 0)
    blocks = draw_blocks(jax.random.fold_in(splits[6], 71), 0)
    user_tile = with_ends(jax.random.randint(splits[2], (LOOPS, COLS, VISITS, SLOTS), 0, UT), jax.random.fold_in(splits[2], 1), 0, UT - 1).astype(jnp.int32)
    item_tile = with_ends(jax.random.randint(splits[3], (LOOPS, COLS, VISITS, SLOTS), 0, IT), jax.random.fold_in(splits[3], 1), 0, IT - 1).astype(jnp.int32)
    ratings = bell_draw(splits[4], (LOOPS, COLS, VISITS, SLOTS, TILE, TILE), 1.0, 6.0, ((0, 4), (1, 32)))
    dest_loop = draw_dest_loop(jax.random.fold_in(splits[6], 71), 0)
    return {"user_factors": user_factors, "blocks": blocks, "user_tile": user_tile, "item_tile": item_tile, "ratings": ratings, "dest_loop": dest_loop}


learn_rate = 0.01
keep_rate = 0.98
highest = lax.Precision.HIGHEST


def residuals(users_here, blocks_here, user_index, item_index, rating_tiles):
    tile_size = rating_tiles.shape[-1]
    rank_width = users_here.shape[-1]
    user_rows = jnp.take(users_here.reshape(-1, tile_size, rank_width), user_index, axis=0)
    item_rows = jnp.take(blocks_here.reshape(-1, tile_size, rank_width), item_index, axis=0)
    guessed = jnp.einsum("kur,kir->kui", user_rows, item_rows, precision=highest)
    return rating_tiles.astype(jnp.float32) - guessed, user_rows, item_rows


def apply_sum(factors, gradients, index):
    groups = factors.size // (gradients.shape[1] * gradients.shape[2])
    tile_hits = (index[None, :] == jnp.arange(groups, dtype=jnp.int32)[:, None]).astype(jnp.float32)
    summed = jnp.einsum("tk,kur->tur", tile_hits, gradients, precision=highest).reshape(factors.shape)
    return factors * keep_rate + learn_rate * summed


def user_update(users_here, errors, item_rows, user_index):
    gradients = jnp.einsum("kui,kir->kur", errors, item_rows, precision=highest)
    return apply_sum(users_here, gradients, user_index)


def item_update(blocks_here, errors, user_rows, item_index):
    gradients = jnp.einsum("kui,kur->kir", errors, user_rows, precision=highest)
    return apply_sum(blocks_here, gradients, item_index)


def ordered_pick(is_live, slot_count):
    flat_live = is_live.reshape(-1).astype(jnp.int32)
    order_rank = (jnp.cumsum(flat_live) - 1).astype(jnp.int32)
    positions = jnp.arange(flat_live.shape[0], dtype=jnp.int32)
    wanted = jnp.arange(slot_count, dtype=jnp.int32)
    chosen = (flat_live[None, :] == 1) & (order_rank[None, :] == wanted[:, None])
    return jnp.sum(jnp.where(chosen, positions[None, :], 0), axis=1).astype(jnp.int32)


def relocate_all(block_grid, dest_loop):
    loop_count, column_count, slot_count = dest_loop.shape
    by_column = jnp.transpose(block_grid, (1, 0, 2, 3, 4)).reshape((column_count, loop_count * slot_count) + block_grid.shape[3:])
    routes_by_column = jnp.transpose(dest_loop, (1, 0, 2))

    def one_column(pieces):
        column_blocks, routes = pieces
        picked = [jnp.take(column_blocks, ordered_pick(routes == target, slot_count), axis=0) for target in range(loop_count)]
        return jnp.stack(picked, axis=0)

    moved = lax.map(one_column, (by_column, routes_by_column))
    return jnp.transpose(moved, (1, 0, 2, 3, 4))


def one_device(pieces):
    users_here, blocks_here, user_index, item_index, rating_tiles = pieces
    errors, user_rows, item_rows = residuals(users_here, blocks_here, user_index, item_index, rating_tiles)
    return user_update(users_here, errors, item_rows, user_index), item_update(blocks_here, errors, user_rows, item_index)


def reference(user_factors, blocks, user_tile, item_tile, ratings, dest_loop):
    devices_all = user_factors.shape[0] * user_factors.shape[1]
    flat_users = user_factors.reshape((devices_all,) + user_factors.shape[2:])
    flat_blocks = blocks.reshape((devices_all,) + blocks.shape[2:])
    flat_user_index = user_tile.reshape((devices_all,) + user_tile.shape[2:])
    flat_item_index = item_tile.reshape((devices_all,) + item_tile.shape[2:])
    flat_ratings = ratings.reshape((devices_all,) + ratings.shape[2:])
    visits = user_tile.shape[2]
    for visit_index in range(visits):
        flat_users, flat_blocks = lax.map(one_device, (flat_users, flat_blocks, flat_user_index[:, visit_index], flat_item_index[:, visit_index], flat_ratings[:, visit_index]))
        block_grid = flat_blocks.reshape(blocks.shape)
        if visit_index == visits // 2 - 1:
            block_grid = relocate_all(block_grid, dest_loop)
        if visit_index < visits - 1:
            block_grid = jnp.roll(block_grid, 1, axis=1)
        flat_blocks = block_grid.reshape(flat_blocks.shape)
    return flat_users.reshape(user_factors.shape), flat_blocks.reshape(blocks.shape)
```

```python
import functools

import jax
import jax.numpy as jnp
from jax import lax
from jax.experimental import pallas as pl
from jax.experimental.pallas import tpu as pltpu
from jax.sharding import PartitionSpec as P


LEARN = 0.01
KEEP = 0.98
CHUNKS = 4
Z_FIRST = ((0, 2), (0, 3), (1, 1), (1, 3))
VMEM = pl.BlockSpec(memory_space=pltpu.VMEM)
SMEM = pl.BlockSpec(memory_space=pltpu.SMEM)
ANY = pl.BlockSpec(memory_space=pl.ANY)


def halves(value):
    high = value.astype(jnp.bfloat16)
    low = (value - high.astype(jnp.float32)).astype(jnp.bfloat16)
    return high, low


def rows_by_rows(a, b):
    return lax.dot_general(a, b, (((1,), (1,)), ((), ())), preferred_element_type=jnp.float32)


def plain(a, b):
    return lax.dot_general(a, b, (((1,), (0,)), ((), ())), preferred_element_type=jnp.float32)


def visit_body(visit, chunk, first, *refs):
    user_ref, item_ref, u_ref, h_ref, r_ref = refs[:5]
    h_out, u_out = refs[-2:]
    u_out[...] = u_ref[...] * KEEP if first else refs[5][...]
    h_out[...] = h_ref[...] * KEEP
    per_block = h_ref.shape[1]
    tiles_of_block = per_block * CHUNKS

    def one_slot(slot, carry):
        item = item_ref[visit, slot]
        user = user_ref[visit, slot]
        block = item // tiles_of_block
        within = item - block * tiles_of_block

        @pl.when(within // per_block == chunk)
        def _():
            tile = within - chunk * per_block
            p_high, p_low = halves(u_ref[user])
            q_high, q_low = halves(h_ref[block, tile])
            guess = (
                rows_by_rows(p_high, q_high)
                + rows_by_rows(p_high, q_low)
                + rows_by_rows(p_low, q_high)
            )
            error = (r_ref[slot].astype(jnp.float32) - guess) * LEARN
            e_high, e_low = halves(error)
            t_high, t_low = halves(error.T)
            u_out[user] += plain(
                jnp.concatenate([e_high, e_high], axis=1), jnp.concatenate([q_high, q_low], axis=0)
            ) + plain(e_low, q_high)
            h_out[block, tile] += plain(
                jnp.concatenate([t_high, t_high], axis=1), jnp.concatenate([p_high, p_low], axis=0)
            ) + plain(t_low, p_high)

        return carry

    lax.fori_loop(0, r_ref.shape[0], one_slot, 0)


def visit_chunk(visit, chunk, tables, users, held, ratings, users_so_far, order=(), whole=None):
    first, in_place = users_so_far is None, whole is not None
    piece = (held.shape[0],) + held.shape[-3:]
    window = pl.BlockSpec((piece[0], None) + piece[1:], lambda _: (0, chunk, 0, 0, 0))
    args = [*tables, users, held, ratings]
    specs = [SMEM, SMEM, VMEM, VMEM if held.ndim == 4 else window]
    specs.append(pl.BlockSpec((None,) + ratings.shape[1:], lambda _: (visit, 0, 0, 0)))
    aliases = {}
    if not first:
        if not (in_place and chunk == CHUNKS - 1):
            aliases[len(args)] = 1
        args.append(users_so_far)
        specs.append(VMEM)
    if in_place and not isinstance(whole, str):
        aliases[len(args)] = 0
        order = (whole, *order)
    args.extend(order)
    specs.extend([ANY] * len(order))
    return pl.pallas_call(
        functools.partial(visit_body, visit, chunk, first),
        grid=(1,),
        out_shape=(
            jax.ShapeDtypeStruct(
                (piece[0], CHUNKS) + piece[1:] if in_place else piece, jnp.float32
            ),
            jax.ShapeDtypeStruct(users.shape, jnp.float32),
        ),
        in_specs=specs,
        out_specs=(window if in_place else VMEM, VMEM),
        input_output_aliases=aliases,
        compiler_params=pltpu.CompilerParams(vmem_limit_bytes=8 << 20),
        cost_estimate=pl.CostEstimate(flops=900000000, bytes_accessed=8 << 20, transcendentals=0),
    )(*args)


def find(routes_ref, side, target, want):
    seen = jnp.int32(0)
    place = jnp.int32(0)
    for position in range(4):
        hit = (routes_ref[2 * side + position // 2, position % 2] == target).astype(jnp.int32)
        place = jnp.where((hit == 1) & (seen == want), jnp.int32(position), place)
        seen = seen + hit
    return place, seen


def pick_into(out_ref, slot, place, core, own_ref, other_ref):
    @pl.when(place // 2 == core)
    def _():
        out_ref[slot] = own_ref[place % 2]

    @pl.when(place // 2 != core)
    def _():
        out_ref[slot] = other_ref[place % 2]


def outgoing_body(routes_ref, own_ref, other_ref, out_ref):
    loop = lax.axis_index("loop")
    side, core = loop // 2, loop % 2
    target = 2 * (1 - side) + core
    for slot in range(2):
        place, _ = find(routes_ref, side, target, slot)
        pick_into(out_ref, slot, place, core, own_ref, other_ref)


def settle_body(routes_ref, own_ref, other_ref, far_ref, *rest):
    out_ref = rest[-1]
    loop = lax.axis_index("loop")
    side, core = loop // 2, loop % 2
    _, from_low = find(routes_ref, 0, loop, 0)
    for slot in range(2):
        in_low = jnp.int32(slot) < from_low
        rank = jnp.where(in_low, jnp.int32(slot), jnp.int32(slot) - from_low)
        near = in_low == (side == 0)
        place, _ = find(routes_ref, side, loop, rank)

        @pl.when(near)
        def _():
            pick_into(out_ref, slot, place, core, own_ref, other_ref)

        @pl.when(jnp.logical_not(near))
        def _():
            out_ref[slot] = far_ref[rank]


def local_move(body, routes, *args, order=()):
    return pl.pallas_call(
        body,
        out_shape=jax.ShapeDtypeStruct(args[0].shape, jnp.float32),
        in_specs=[SMEM] + [VMEM] * len(args) + [ANY] * len(order),
        out_specs=VMEM,
        compiler_params=pltpu.CompilerParams(vmem_limit_bytes=6 << 20),
        cost_estimate=pl.CostEstimate(flops=0, bytes_accessed=2 << 20, transcendentals=0),
    )(routes, *args, *order)


def next_shard(value):
    count = lax.axis_size("blk")
    return lax.ppermute(value, "blk", [(at, (at + 1) % count) for at in range(count)])


def next_shard_by_z_first(value):
    count = lax.axis_size("blk")
    ends = {count // 2 - 1: count - 1, count - 1: count // 2 - 1}
    value = lax.ppermute(value, "blk", [(at, ends.get(at, at)) for at in range(count)])
    return lax.ppermute(value, "blk", [(ends.get(at, at), (at + 1) % count) for at in range(count)])


def across(chunk, routes):
    other = lax.ppermute(chunk, "loop", [(at, at ^ 1) for at in range(4)])
    outgoing = local_move(outgoing_body, routes, chunk, other)
    far = lax.ppermute(outgoing, "loop", [(at, at ^ 2) for at in range(4)])
    return chunk, other, far


def on_device(user_factors, blocks, user_tile, item_tile, ratings, dest_loop):
    routes = dest_loop[:, 0, :]
    tables = (user_tile[0, 0], item_tile[0, 0])
    visits = tables[0].shape[0]
    tile, rank = ratings.shape[-1], user_factors.shape[-1]
    rating_tiles = ratings[0, 0]
    users = user_factors.reshape(-1, tile, rank)
    start = blocks.reshape(blocks.shape[2], CHUNKS, -1, tile, rank)
    pieces = [start] * CHUNKS
    move_at = visits // 2 - 1
    for visit in range(visits):
        so_far, whole = None, "new" if visit == visits - 1 else None
        for at in range(CHUNKS):
            after, so_far = visit_chunk(
                visit, at, tables, users, pieces[at], rating_tiles, so_far, (), whole
            )
            if visit == move_at:
                moving = across(after, routes)
                after = local_move(settle_body, routes, *moving)
            if visit == visits - 1:
                whole = after
            elif (visit, at) in Z_FIRST:
                pieces[at] = next_shard_by_z_first(after)
            else:
                pieces[at] = next_shard(after)
        users = so_far
    return (users.reshape(user_factors.shape), whole.reshape(blocks.shape))


def solution(mesh):
    placed = (
        P("loop", "blk", None, None),
        P("loop", "blk", None, None, None),
        P("loop", "blk", None, None),
        P("loop", "blk", None, None),
        P("loop", "blk", None, None, None, None),
        P(None, "blk", None),
    )

    return jax.shard_map(
        on_device,
        mesh=mesh,
        in_specs=placed,
        out_specs=(P("loop", "blk", None, None), P("loop", "blk", None, None, None)),
        check_vma=False,
    )
```

```python
import functools

import jax
import jax.numpy as jnp
from jax import lax
from jax.experimental import pallas as pl
from jax.experimental.pallas import tpu as pltpu
from jax.sharding import PartitionSpec as P


LEARN = 0.01
KEEP = 0.98
CHUNKS = 4
AROUND = {(1, 1): 5, (1, 2): 1}
Z_FIRST = ((0, 2), (0, 3))
LONG_WAY = ((2, 0),)
ROW = 4
LAST_ORDER = (1, 2, 0, 3)
VMEM = pl.BlockSpec(memory_space=pltpu.VMEM)
SMEM = pl.BlockSpec(memory_space=pltpu.SMEM)
ANY = pl.BlockSpec(memory_space=pl.ANY)


def both(value):
    high = value.astype(jnp.bfloat16)
    low = (value - high.astype(jnp.float32)).astype(jnp.bfloat16)
    return jnp.concatenate([high, low], axis=0)


def rows_by_rows(a, b):
    return lax.dot_general(a, b, (((1,), (1,)), ((), ())), preferred_element_type=jnp.float32)


def plain(a, b):
    return lax.dot_general(a, b, (((1,), (0,)), ((), ())), preferred_element_type=jnp.float32)


def accumulate(visit, chunk, user_ref, item_ref, u_ref, h_ref, r_ref, h_out, u_out):
    per_block = h_ref.shape[1]
    tiles_of_block = per_block * CHUNKS
    rows = h_ref.shape[2]

    def summed(value):
        return value[:rows] + value[rows:]

    def one_slot(slot, carry):
        item = item_ref[visit, slot]
        user = user_ref[visit, slot]
        block = item // tiles_of_block
        within = item - block * tiles_of_block

        @pl.when(within // per_block == chunk)
        def _():
            tile = within - chunk * per_block
            p, q = both(u_ref[user]), both(h_ref[block, tile])
            guess = rows_by_rows(p, q)
            guess = guess[:rows, :rows] + guess[:rows, rows:] + guess[rows:, :rows]
            error = (r_ref[visit, slot].astype(jnp.float32) - guess) * LEARN
            e, t = both(error), both(error.T)
            u_out[user] += summed(plain(jnp.concatenate([e, e], axis=1), q))
            h_out[block, tile] += summed(plain(jnp.concatenate([t, t], axis=1), p))

        return carry

    lax.fori_loop(0, r_ref.shape[1], one_slot, 0)


def opening_body(*refs):
    user_hbm, item_hbm, u_hbm, h_hbm, r_hbm = refs[:5]
    h_out, u_out, u_ref, h_ref, r_ref, user_ref, item_ref, sems = refs[5:]
    copies = [
        pltpu.make_async_copy(user_hbm, user_ref, sems.at[0]),
        pltpu.make_async_copy(item_hbm, item_ref, sems.at[1]),
        pltpu.make_async_copy(h_hbm.at[:, 0], h_ref.at[0], sems.at[2]),
        pltpu.make_async_copy(u_hbm, u_ref, sems.at[3]),
        pltpu.make_async_copy(r_hbm.at[0], r_ref.at[0], sems.at[4]),
    ]
    count = len(copies)
    later = [
        pltpu.make_async_copy(h_hbm.at[:, at], h_ref.at[at], sems.at[count + at - 1])
        for at in range(1, CHUNKS)
    ]
    count += len(later)
    later.append(pltpu.make_async_copy(r_hbm.at[1:], r_ref.at[1:], sems.at[count]))
    for copy in copies + later:
        copy.start()
    for copy in copies:
        copy.wait()
    u_out[...] = u_ref[...] * KEEP
    h_out[...] = h_ref[0] * KEEP
    accumulate(0, 0, user_ref, item_ref, u_ref, h_ref.at[0], r_ref, h_out, u_out)
    for copy in later:
        copy.wait()


def kernel_params(size):
    return dict(
        compiler_params=pltpu.CompilerParams(vmem_limit_bytes=size << 20),
        cost_estimate=pl.CostEstimate(flops=900000000, bytes_accessed=8 << 20, transcendentals=0),
    )


def opening(tables, users, blocks, ratings):
    piece = (blocks.shape[0],) + blocks.shape[2:]
    hbm = pl.BlockSpec(memory_space=pltpu.HBM)
    return pl.pallas_call(
        opening_body,
        out_shape=(
            jax.ShapeDtypeStruct(piece, jnp.float32),
            jax.ShapeDtypeStruct(users.shape, jnp.float32),
            jax.ShapeDtypeStruct(users.shape, jnp.float32),
            jax.ShapeDtypeStruct((CHUNKS,) + piece, jnp.float32),
            jax.ShapeDtypeStruct(ratings.shape, ratings.dtype),
        ),
        in_specs=[hbm] * 5,
        out_specs=(VMEM,) * 5,
        scratch_shapes=[
            pltpu.SMEM(tables[0].shape, jnp.int32),
            pltpu.SMEM(tables[1].shape, jnp.int32),
            pltpu.SemaphoreType.DMA((5 + CHUNKS,)),
        ],
        name="visit0_0",
        **kernel_params(6),
    )(*[pltpu.with_memory_space_constraint(x, pltpu.HBM) for x in (*tables, users, blocks, ratings)])


def visit_body(visit, chunk, first, kind, *refs):
    refs = list(refs)
    user_ref, item_ref, u_ref, r_ref = refs[:4]
    del refs[:4]
    so_far = None if first else refs.pop(0)
    h_ref = refs.pop(0)
    if kind == "all":
        h_ref = h_ref.at[chunk]
    if kind == "two":
        other_ref, scratch = refs.pop(0), refs.pop()
        half = lax.axis_size("blk") // 2
        is_start = lax.rem(lax.axis_index("blk"), half) == 0

        @pl.when(is_start)
        def _():
            scratch[...] = other_ref[...]

        @pl.when(jnp.logical_not(is_start))
        def _():
            scratch[...] = h_ref[...]

        h_ref = scratch
    h_out, u_out = refs[-2:]
    u_out[...] = u_ref[...] * KEEP if first else so_far[...]
    h_out[...] = h_ref[...] * KEEP
    accumulate(visit, chunk, user_ref, item_ref, u_ref, h_ref, r_ref, h_out, u_out)


def visit_chunk(visit, chunk, tables, users, held, ratings, so_far, whole=None):
    first, in_place = so_far is None, whole is not None
    kind = "two" if isinstance(held, tuple) else "all" if held.ndim == 5 else "one"
    held = held if kind == "two" else (held,)
    piece = held[0].shape[-4:]
    window = pl.BlockSpec((piece[0], None) + piece[1:], lambda _: (0, chunk, 0, 0, 0))
    args = [*tables, users, ratings]
    specs = [SMEM, SMEM, VMEM, VMEM]
    aliases = {}
    if not first:
        if not (in_place and chunk == LAST_ORDER[-1]):
            aliases[len(args)] = 1
        args.append(so_far)
        specs.append(VMEM)
    args.extend(held)
    specs.extend([VMEM] * len(held))
    if in_place and not isinstance(whole, str):
        aliases[len(args)] = 0
        args.append(whole)
        specs.append(ANY)
    return pl.pallas_call(
        functools.partial(visit_body, visit, chunk, first, kind),
        grid=(1,),
        out_shape=(
            jax.ShapeDtypeStruct(
                (piece[0], CHUNKS) + piece[1:] if in_place else piece, jnp.float32
            ),
            jax.ShapeDtypeStruct(users.shape, jnp.float32),
        ),
        in_specs=specs,
        out_specs=(window if in_place else VMEM, VMEM),
        scratch_shapes=[pltpu.VMEM(piece, jnp.float32)] if kind == "two" else [],
        input_output_aliases=aliases,
        **kernel_params(8),
    )(*args)


def find(routes_ref, side, target, want):
    seen = jnp.int32(0)
    place = jnp.int32(0)
    for position in range(4):
        hit = (routes_ref[position % 2, 2 * side + position // 2] == target).astype(jnp.int32)
        place = jnp.where((hit == 1) & (seen == want), jnp.int32(position), place)
        seen = seen + hit
    return place, seen


def pick_into(out_ref, slot, place, core, own_ref, other_ref):
    @pl.when(place // 2 == core)
    def _():
        out_ref[slot] = own_ref[place % 2]

    @pl.when(place // 2 != core)
    def _():
        out_ref[slot] = other_ref[place % 2]


def outgoing_body(routes_ref, own_ref, other_ref, out_ref):
    loop = lax.axis_index("loop")
    side, core = loop // 2, loop % 2
    target = 2 * (1 - side) + core
    for slot in range(2):
        place, _ = find(routes_ref, side, target, slot)
        pick_into(out_ref, slot, place, core, own_ref, other_ref)


def settle_body(routes_ref, own_ref, other_ref, far_ref, *rest):
    out_ref = rest[-1]
    loop = lax.axis_index("loop")
    side, core = loop // 2, loop % 2
    _, from_low = find(routes_ref, 0, loop, 0)
    for slot in range(2):
        in_low = jnp.int32(slot) < from_low
        rank = jnp.where(in_low, jnp.int32(slot), jnp.int32(slot) - from_low)
        near = in_low == (side == 0)
        place, _ = find(routes_ref, side, loop, rank)

        @pl.when(near)
        def _():
            pick_into(out_ref, slot, place, core, own_ref, other_ref)

        @pl.when(jnp.logical_not(near))
        def _():
            out_ref[slot] = far_ref[rank]


def local_move(body, routes, *args, order=()):
    return pl.pallas_call(
        body,
        out_shape=jax.ShapeDtypeStruct(args[0].shape, jnp.float32),
        in_specs=[SMEM] + [VMEM] * len(args) + [ANY] * len(order),
        out_specs=VMEM,
        compiler_params=pltpu.CompilerParams(vmem_limit_bytes=6 << 20),
        cost_estimate=pl.CostEstimate(flops=0, bytes_accessed=2 << 20, transcendentals=0),
    )(routes, *args, *order)


def next_shard(value):
    count = lax.axis_size("blk")
    return lax.ppermute(value, "blk", [(at, (at + 1) % count) for at in range(count)])


def next_shard_long_way(value):
    count = lax.axis_size("blk")

    def before(at):
        return at - at % ROW + (at - 1) % ROW

    def before_in_next(at):
        return before(at) if (at + 1) % ROW else (at + 1) % count + ROW - 2

    for goal in (before_in_next, before, before):
        value = lax.ppermute(value, "blk", [(at, goal(at)) for at in range(count)])
    return value


def next_shard_z_first(value):
    count = lax.axis_size("blk")
    ends = {count // 2 - 1: count - 1, count - 1: count // 2 - 1}
    value = lax.ppermute(value, "blk", [(at, ends.get(at, at)) for at in range(count)])
    return lax.ppermute(value, "blk", [(ends.get(at, at), (at + 1) % count) for at in range(count)])


def next_shard_around(value, mid):
    count = lax.axis_size("blk")
    half = count // 2
    near = lax.ppermute(
        value, "blk", [(at, at + 1) for at in range(count) if (at + 1) % half]
    )
    value = lax.ppermute(value, "blk", [(half - 1, half + mid), (count - 1, mid)])
    return near, lax.ppermute(value, "blk", [(half + mid, half), (mid, 0)])


def across(chunk, routes):
    other = lax.ppermute(chunk, "loop", [(at, at ^ 1) for at in range(4)])
    outgoing = local_move(outgoing_body, routes, chunk, other)
    far = lax.ppermute(outgoing, "loop", [(at, at ^ 2) for at in range(4)])
    return chunk, other, far


def on_device(user_factors, blocks, user_tile, item_tile, ratings, dest_loop):
    routes = dest_loop.transpose(1, 2, 0)[0]
    tables = (user_tile[0, 0], item_tile[0, 0])
    visits = tables[0].shape[0]
    tile, rank = ratings.shape[-1], user_factors.shape[-1]
    users = user_factors.reshape(-1, tile, rank)
    held = blocks.reshape(blocks.shape[2], CHUNKS, -1, tile, rank)
    move_at = visits // 2 - 1
    for visit in range(visits):
        so_far, whole = None, "new" if visit == visits - 1 else None
        order = LAST_ORDER if visit == visits - 1 else range(CHUNKS)
        for at in order:
            if (visit, at) == (0, 0):
                after, so_far, users, held, rating_tiles = opening(
                    tables, users, held, ratings[0, 0]
                )
                pieces = [held] * CHUNKS
            else:
                after, so_far = visit_chunk(
                    visit, at, tables, users, pieces[at], rating_tiles, so_far, whole
                )
            if visit == move_at:
                moving = across(after, routes)
                after = local_move(settle_body, routes, *moving)
            if visit == visits - 1:
                whole = after
            elif (visit, at) in AROUND:
                pieces[at] = next_shard_around(after, AROUND[visit, at])
            elif (visit, at) in Z_FIRST:
                pieces[at] = next_shard_z_first(after)
            elif (visit, at) in LONG_WAY:
                pieces[at] = next_shard_long_way(after)
            else:
                pieces[at] = next_shard(after)
        users = so_far
    return (users.reshape(user_factors.shape), whole.reshape(blocks.shape))


def solution(mesh):
    placed = (
        P("loop", "blk", None, None),
        P("loop", "blk", None, None, None),
        P("loop", "blk", None, None),
        P("loop", "blk", None, None),
        P("loop", "blk", None, None, None, None),
        P(None, "blk", None),
    )

    return jax.shard_map(
        on_device,
        mesh=mesh,
        in_specs=placed,
        out_specs=(P("loop", "blk", None, None), P("loop", "blk", None, None, None)),
        check_vma=False,
    )
```
